1024 devices in a mesh: dom: 64 (over x, z), sub: 16 (over y, core).
Axes of the slice: x: 8, y: 8, z: 8, core: 2. Of those that a mesh axis runs over, the one named last changes fastest.
Arguments:
- a_blocks: bfloat16 [64, 768, 8, 64, 64], P('dom', 'sub'), may hold values from -0.25 to 0.25
- p_blocks: bfloat16 [64, 768, 64, 64], P('dom', 'sub'), may hold values from -2.09375 to 2.09375
- a_cols: int32 [64, 768, 8], P('dom', 'sub'), may hold values from 0 to 143
- tile_of_item: int32 [64, 768, 8], P('dom', 'sub'), may hold values from 0 to 191, as said below
Outputs:
- coarse: bfloat16 [64, 192, 64, 64], P('dom')
The draws below stay inside these ranges and needn't reach their ends.
Inputs may be any that keep to these rules, and one draw needn't show every extreme that they name: `tile_of_item`: within one partition, the blocks held by one device name at most 8 distinct tiles of each sub index, and exactly 8 of some sub index.
All inputs are finite; a program needn't handle non-finite values.
Results may differ from the reference program's by a relative error of at most 0.0049.
Values may be sent and summed in bfloat16 or wider, within the bound.
No kernel may reach another device: no remote copies, remote signals or barrier semaphores. Data moves between devices by JAX's collectives and lax.ppermute only.
A program may use at most 64 MiB of HBM per device.

```python
import jax
import jax.numpy as jnp
from jax import lax

BS = 64
FB = 48
KA = 8
CAP = 8
CB = 2
KC = 6
FROWS = 768
N_DOM = 64
N_SUB = 16


def draw_tile_of_item(key, part):
    own = CB * KC
    count = FB * KA

    def device(dkey):
        keys = jax.random.split(dkey, 5)
        loads = jax.random.randint(keys[0], (N_SUB,), 1, CAP + 1)
        fullest = jax.random.randint(keys[1], (), 0, N_SUB)
        loads = jnp.where(jnp.arange(N_SUB) == fullest, CAP, loads)
        orders = jax.vmap(lambda k: jax.random.permutation(k, own))(jax.random.split(keys[2], N_SUB))
        tiles = jnp.arange(N_SUB, dtype=jnp.int32)[:, None] * own + orders[:, :CAP].astype(jnp.int32)
        valid = jnp.arange(CAP)[None, :] < loads[:, None]
        ranked = jnp.argsort(jnp.where(valid.reshape(-1), 0, 1), stable=True)
        total = jnp.sum(loads)
        position = jnp.arange(count)
        pick = jnp.where(position < total, position, jax.random.randint(keys[3], (count,), 0, total))
        chosen = tiles.reshape(-1)[ranked[pick]]
        return chosen[jax.random.permutation(keys[4], count)].astype(jnp.int32)
    result = jax.vmap(device)(jax.random.split(key, N_DOM * N_SUB))
    return result.reshape(N_DOM, N_SUB * FB, KA)


def touch_ends(array, own_key, smallest, largest):
    shape = array.shape
    spot = [jax.random.randint(jax.random.fold_in(own_key, axis), (), 0, shape[axis]) for axis in range(len(shape))]
    array = array.at[tuple(spot)].set(smallest)
    longest = shape.index(max(shape))
    spot[longest] = (spot[longest] + 1) % shape[longest]
    return array.at[tuple(spot)].set(largest)


def steps_of(rng, extent, shards, least, top_value):
    loudness = 1.0
    for axis_at, parts in shards:
        heights = jax.random.uniform(jax.random.fold_in(jax.random.fold_in(rng, 6), axis_at), (parts,), jnp.float32, least / len(shards), top_value / len(shards))
        loudness = loudness * jnp.repeat(jnp.exp(heights), extent[axis_at] // parts).reshape((-1,) + (1,) * (len(extent) - 1 - axis_at))
    return loudness


def bell_draw(stream_key, shape, width, limit, cuts=(), kind=jnp.bfloat16):
    values = width * jax.random.normal(stream_key, shape, jnp.float32)
    if cuts:
        values = values * steps_of(stream_key, shape, cuts, -0.22, 0.18)
    return jnp.clip(values, -limit, limit).astype(kind)


def setup_inputs(seed: int = 0) -> dict:
    seeds = jax.random.split(jax.random.key(seed), 5)
    return {
        "a_blocks": bell_draw(seeds[0], (N_DOM, FROWS, KA, BS, BS), (BS * KA) ** -0.5, 0.25, ((0, 64), (1, 16))),
        "p_blocks": bell_draw(seeds[1], (N_DOM, FROWS, BS, BS), 0.35, 2.09375, ((0, 64), (1, 16))),
        "a_cols": touch_ends(jax.random.randint(seeds[2], (N_DOM, FROWS, KA), 0, 3 * FB), jax.random.fold_in(seeds[2], 1), 0, (3 * FB) - 1).astype(jnp.int32),
        "tile_of_item": draw_tile_of_item(jax.random.fold_in(seeds[4], 71), 0),
    }


def reference(a_blocks, p_blocks, a_cols, tile_of_item):
    zero_rim = jnp.zeros((1,) + p_blocks.shape[1:], p_blocks.dtype)
    padded = jnp.concatenate([zero_rim, p_blocks, zero_rim], axis=0)

    def one_part(index):
        near = lax.dynamic_slice_in_dim(padded, index, 3, 0)
        near = near.reshape(3, N_SUB, FB, BS, BS).transpose(1, 0, 2, 3, 4).reshape(N_SUB, 3 * FB, BS, BS)
        blocks = lax.dynamic_index_in_dim(a_blocks, index, 0, False).reshape(N_SUB, FB, KA, BS, BS)
        cols = lax.dynamic_index_in_dim(a_cols, index, 0, False).reshape(N_SUB, FB * KA)
        ghost = jax.vmap(lambda table, where_to: jnp.take(table, where_to, axis=0))(near, cols)
        ghost = ghost.reshape(N_SUB, FB, KA, BS, BS)
        product = jnp.einsum("sikab,sikbc->sikac", blocks.astype(jnp.float32), ghost.astype(jnp.float32))
        product = lax.optimization_barrier(product.astype(jnp.bfloat16)).astype(jnp.float32)
        own_rows = lax.dynamic_index_in_dim(p_blocks, index, 0, False).reshape(N_SUB, FB, BS, BS)
        terms = jnp.einsum("siba,sikbc->sikac", own_rows.astype(jnp.float32), product)
        tiles = lax.dynamic_index_in_dim(tile_of_item, index, 0, False).reshape(-1)
        summed = jax.ops.segment_sum(terms.reshape(-1, BS, BS), tiles, N_SUB * CB * KC)
        return summed.astype(jnp.bfloat16)

    return lax.map(one_part, jnp.arange(N_DOM, dtype=jnp.int32))
```

```python
import functools

import jax
import jax.numpy as jnp
from jax import lax
from jax.experimental import pallas as pl
from jax.experimental.pallas import tpu as pltpu
from jax.sharding import PartitionSpec as P

F32, BF16 = jnp.float32, jnp.bfloat16
ROWS = 8


def twice(x):
    return jnp.concatenate([x, x], axis=-1)


def galerkin(chip_core, cols, tiles, a_ref, p_ref, before_ref, after_ref, keep_ref, send_ref, near, acc):
    fine, width = p_ref.shape[0], p_ref.shape[1]
    half = fine // 2
    steps, own = pl.num_programs(0), pl.program_id(0)
    n_tiles = acc.shape[0] // width

    @pl.when(own == 0)
    def _():
        def clear(t, _):
            acc[pl.ds(pl.multiple_of(t * width, width), width), :] = jnp.zeros((width, 2 * width), F32)
            return 0

        lax.fori_loop(0, n_tiles, clear, 0, unroll=4)

        def fill(r, _):
            near[fine + r] = twice(p_ref[r])
            return 0

        lax.fori_loop(0, fine, fill, 0, unroll=4)

        def fill_ghost(r, _):
            for at, ref in ((0, before_ref), (2 * fine, after_ref)):
                both = ref[r]
                near[at + r] = twice(both[:, :width])
                near[at + half + r] = twice(both[:, width:])
            return 0

        lax.fori_loop(0, half, fill_ghost, 0, unroll=2)

    per_row = a_ref.shape[1]

    def one_row(r, _):
        i = own * ROWS + r
        left = p_ref[i].T
        terms = []
        for k in range(per_row):
            ap = jnp.dot(a_ref[r, k], near[cols[k, i]], preferred_element_type=F32).astype(BF16)
            terms.append(jnp.dot(left, ap, preferred_element_type=F32))
        for k in range(per_row):
            at = pl.ds(pl.multiple_of(tiles[k, i] * width, width), width)
            acc[at, :] += terms[k]
        return 0

    lax.fori_loop(0, ROWS, one_row, 0)

    @pl.when(own == steps - 1)
    def _():
        core = chip_core[0]
        low = lax.broadcasted_iota(jnp.int32, (n_tiles, 2 * width), 1) < width
        groups = keep_ref.shape[0]
        rows = width // (2 * groups)

        def pair(a):
            even = acc[pl.ds(a, n_tiles, stride=width), :]
            odd = acc[pl.ds(a + 1, n_tiles, stride=width), :]
            return jnp.where(low, even, odd)

        for y in range(groups):
            for p in range(rows // 2):
                base = 2 * rows * y + 2 * p
                at = slice(p * n_tiles, (p + 1) * n_tiles)
                keep_ref[y, at, :] = pair(base + rows * core)
                send_ref[y, at, :] = pair(base + rows * (1 - core)).astype(BF16)


def finish(got_ref, out_ref):
    peers, packed, lanes = got_ref.shape
    n_tiles = packed // 2
    total = got_ref[0].astype(F32)
    for y in range(1, peers):
        total = total + got_ref[y].astype(F32)
    first, second = total[:n_tiles], total[n_tiles:]
    rest = jnp.concatenate([first[lanes:], second[lanes:]], axis=0)
    block = jnp.concatenate([first[:lanes].T, second[:lanes].T, rest.T], axis=0).astype(BF16)
    for y in range(peers):
        out_ref[y] = block


def spread(chip_core, mine_ref, other_ref, out_ref):
    core = chip_core[0]
    packed, lanes = mine_ref.shape[1], mine_ref.shape[2]
    slab, half = out_ref.shape[0] // 2, lanes // 2
    for ref, at in ((mine_ref, core), (other_ref, 1 - core)):
        start = pl.multiple_of(at * slab, slab)
        out_ref[pl.ds(start, slab), 0:lanes] = ref[0, 0:slab, :]
        rest = ref[0, slab:packed, :]
        out_ref[pl.ds(start, lanes), lanes : lanes + half] = rest[:, :half]
        out_ref[pl.ds(start + lanes, lanes), lanes : lanes + half] = rest[:, half:]


def body(n_tiles, a_blocks, p_blocks, a_cols, tile_of_item):
    fine, per_row, width = a_blocks.shape[1], a_blocks.shape[2], a_blocks.shape[3]
    subs, doms = lax.axis_size("sub"), lax.axis_size("dom")
    chips = subs // 2
    lanes = 2 * width
    half = fine // 2
    core = (lax.axis_index("sub") % 2).astype(jnp.int32).reshape(1)
    own = p_blocks[0]
    cols, tiles = a_cols[0].T, tile_of_item[0].T

    up = [(d, d + 1) for d in range(doms - 1)]
    down = [(d + 1, d) for d in range(doms - 1)]
    swap = [(s, s ^ 1) for s in range(subs)]
    columns = [[2 * y + c for y in range(chips)] for c in range(2)]

    packed = jnp.concatenate([own[:half], own[half:]], axis=-1)
    before = lax.ppermute(packed, "dom", up)
    after = lax.ppermute(packed, "dom", down)

    whole = lambda shape: pl.BlockSpec(shape, lambda *_: (0,) * len(shape))
    share = width // subs // 2 * n_tiles
    keep, send = pl.pallas_call(
        galerkin,
        out_shape=(
            jax.ShapeDtypeStruct((chips, share, lanes), F32),
            jax.ShapeDtypeStruct((chips, share, lanes), BF16),
        ),
        grid_spec=pltpu.PrefetchScalarGridSpec(
            num_scalar_prefetch=3,
            grid=(fine // ROWS,),
            in_specs=[
                pl.BlockSpec((ROWS, per_row, width, width), lambda g, *_: (g, 0, 0, 0)),
                whole((fine, width, width)),
                whole((half, width, lanes)),
                whole((half, width, lanes)),
            ],
            out_specs=(whole((chips, share, lanes)), whole((chips, share, lanes))),
            scratch_shapes=[
                pltpu.VMEM((3 * fine, width, lanes), BF16),
                pltpu.VMEM((n_tiles * width, lanes), F32),
            ],
        ),
        name="galerkin",
    )(core, cols, tiles, a_blocks[0], own, before, after)

    other = lax.ppermute(send, "sub", swap)
    merged = (keep + other.astype(F32)).astype(BF16)
    got = lax.all_to_all(merged, "sub", 0, 0, axis_index_groups=columns, tiled=True)
    block = pl.pallas_call(
        finish, out_shape=jax.ShapeDtypeStruct((chips, share, lanes), BF16), name="finish"
    )(got)
    mine = lax.all_to_all(block, "sub", 0, 0, axis_index_groups=columns, tiled=True)
    theirs = lax.ppermute(mine, "sub", swap)
    slab = width * width // chips
    spec = pl.BlockSpec((1, share, lanes), lambda y, *_: (y, 0, 0))
    out = pl.pallas_call(
        spread,
        out_shape=jax.ShapeDtypeStruct((width * width, n_tiles), BF16),
        grid_spec=pltpu.PrefetchScalarGridSpec(
            num_scalar_prefetch=1,
            grid=(chips,),
            in_specs=[spec, spec],
            out_specs=pl.BlockSpec((slab, n_tiles), lambda y, *_: (y, 0)),
        ),
        name="spread",
    )(core, mine, theirs)
    return out.reshape(width, width, n_tiles).transpose(2, 0, 1)[None]


def solution(mesh):
    placed = (
        P("dom", "sub", None, None, None),
        P("dom", "sub", None, None),
        P("dom", "sub", None),
        P("dom", "sub", None),
    )
    n_tiles = 12 * mesh.shape["sub"]
    return jax.shard_map(
        functools.partial(body, n_tiles),
        mesh=mesh,
        in_specs=placed,
        out_specs=P("dom", None, None, None),
        check_vma=False,
    )
```

```python
import functools

import jax
import jax.numpy as jnp
from jax import lax
from jax.experimental import pallas as pl
from jax.experimental.pallas import tpu as pltpu
from jax.sharding import PartitionSpec as P

F32, BF16 = jnp.float32, jnp.bfloat16
ROWS = 8
UNROLL = 8


def twice(x):
    return jnp.concatenate([x, x], axis=-1)


def galerkin(chip_core, cols, tiles, a_ref, p_ref, before_ref, after_ref, keep_ref, send_ref, near, acc):
    fine, width = p_ref.shape[0], p_ref.shape[1]
    half = fine // 2
    steps, own = pl.num_programs(0), pl.program_id(0)
    n_tiles = acc.shape[0] // width

    @pl.when(own == 0)
    def _():
        def clear(t, _):
            acc[pl.ds(pl.multiple_of(t * width, width), width), :] = jnp.zeros((width, 2 * width), F32)
            return 0

        lax.fori_loop(0, n_tiles, clear, 0, unroll=4)

        def fill(r, _):
            near[fine + r] = twice(p_ref[r])
            return 0

        lax.fori_loop(0, fine, fill, 0, unroll=4)

        def fill_ghost(r, _):
            for at, ref in ((0, before_ref), (2 * fine, after_ref)):
                both = ref[r]
                near[at + r] = twice(both[:, :width])
                near[at + half + r] = twice(both[:, width:])
            return 0

        lax.fori_loop(0, half, fill_ghost, 0, unroll=2)

    per_row = a_ref.shape[1]

    def one_row(r, _):
        i = own * ROWS + r
        left = p_ref[i].T
        terms = []
        for k in range(0, per_row, 2):
            ap = [
                jnp.dot(a_ref[r, q], near[cols[q, i]], preferred_element_type=F32).astype(BF16)
                for q in (k, k + 1)
            ]
            both = jnp.dot(left, jnp.concatenate(ap, axis=1), preferred_element_type=F32)
            terms += [both[:, : 2 * width], both[:, 2 * width :]]
        for k in range(per_row):
            at = pl.ds(pl.multiple_of(tiles[k, i] * width, width), width)
            acc[at, :] += terms[k]
        return 0

    lax.fori_loop(0, ROWS, one_row, 0, unroll=UNROLL)

    @pl.when(own == steps - 1)
    def _():
        first_core = lax.broadcasted_iota(jnp.int32, (8, 2 * width), 0) * 0 + chip_core[0] == 0
        left_half = lax.broadcasted_iota(jnp.int32, (8, 2 * width), 1) < width
        upper = lax.broadcasted_iota(jnp.int32, (8, 2 * width), 0) < 4
        groups, quads = keep_ref.shape[0], n_tiles // 4

        def pack(u, _):
            for y in range(groups):
                rows = []
                for w in range(2):
                    def tile(q):
                        start = (2 * u + w + q * quads) * width + 8 * y
                        return acc[pl.ds(pl.multiple_of(start, 8), 8), :]

                    even = jnp.where(left_half, tile(0), tile(2))
                    odd = jnp.where(left_half, tile(1), tile(3))
                    top = jnp.where(upper, even, pltpu.roll(odd, 4, 0))
                    bottom = jnp.where(upper, pltpu.roll(even, 4, 0), odd)
                    rows.append((jnp.where(first_core, top, bottom), jnp.where(first_core, bottom, top)))
                at = pl.ds(pl.multiple_of(16 * u, 16), 16)
                keep_ref[y, at, :] = jnp.concatenate([rows[0][0], rows[1][0]], axis=0)
                send_ref[y, at, :] = jnp.concatenate([rows[0][1], rows[1][1]], axis=0).astype(BF16)
            return 0

        lax.fori_loop(0, quads // 2, pack, 0, unroll=2)


def finish(got_ref, out_ref, total):
    peers, packed, lanes = got_ref.shape
    half, quads = lanes // 2, packed // 8
    n_tiles = 4 * quads
    sums = got_ref[0].astype(F32)
    for y in range(1, peers):
        sums = sums + got_ref[y].astype(F32)
    total[...] = sums
    slab = []
    for r in range(4):
        rows = [total[pl.ds(4 * s + r, quads, stride=8), :] for s in range(2)]
        turned = jnp.concatenate(rows, axis=0).T
        slab.append(jnp.concatenate([turned[:half], turned[half:]], axis=1))
    slab = jnp.concatenate(slab, axis=0)
    rest = jnp.concatenate([slab[:lanes, lanes:], slab[lanes:, lanes:]], axis=1)
    block = jnp.concatenate([slab[:, :lanes], rest], axis=0).astype(BF16)
    for y in range(peers):
        out_ref[y] = block


def spread(mine_hbm, other_hbm, out_hbm, mine, other, out, got_sem, put_sem):
    core = lax.axis_index("sub") % 2
    chips, packed, lanes = mine.shape
    slab, half = out.shape[0] // (2 * chips), lanes // 2
    fetch = lambda y: [
        pltpu.make_async_copy(src.at[y], dst.at[y], got_sem.at[i, y])
        for i, (src, dst) in enumerate(((mine_hbm, mine), (other_hbm, other)))
    ]
    put = lambda y: pltpu.make_async_copy(
        out.at[pl.ds(2 * slab * y, 2 * slab)], out_hbm.at[pl.ds(2 * slab * y, 2 * slab)], put_sem.at[y]
    )
    for y in range(chips):
        for copy in fetch(y):
            copy.start()
    for y in range(chips):
        for copy, ref, at in zip(fetch(y), (mine, other), (core, 1 - core)):
            copy.wait()
            start = pl.multiple_of((2 * y + at) * slab, slab)
            out[pl.ds(start, slab), 0:lanes] = ref[y, 0:slab, :]
            rest = ref[y, slab:packed, :]
            out[pl.ds(start, lanes), lanes : lanes + half] = rest[:, :half]
            out[pl.ds(start + lanes, lanes), lanes : lanes + half] = rest[:, half:]
        put(y).start()
    for y in range(chips):
        put(y).wait()


def body(n_tiles, a_blocks, p_blocks, a_cols, tile_of_item):
    fine, per_row, width = a_blocks.shape[1], a_blocks.shape[2], a_blocks.shape[3]
    subs, doms = lax.axis_size("sub"), lax.axis_size("dom")
    chips = subs // 2
    lanes = 2 * width
    half = fine // 2
    core = (lax.axis_index("sub") % 2).astype(jnp.int32).reshape(1)
    own = p_blocks[0]
    cols, tiles = a_cols[0].T, tile_of_item[0].T

    up = [(d, d + 1) for d in range(doms - 1)]
    down = [(d + 1, d) for d in range(doms - 1)]
    swap = [(s, s ^ 1) for s in range(subs)]
    columns = [[2 * y + c for y in range(chips)] for c in range(2)]

    packed = jnp.concatenate([own[:half], own[half:]], axis=-1)
    before = lax.ppermute(packed, "dom", up)
    after = lax.ppermute(packed, "dom", down)

    whole = lambda shape: pl.BlockSpec(shape, lambda *_: (0,) * len(shape))
    share = width // subs // 2 * n_tiles
    keep, send = pl.pallas_call(
        galerkin,
        out_shape=(
            jax.ShapeDtypeStruct((chips, share, lanes), F32),
            jax.ShapeDtypeStruct((chips, share, lanes), BF16),
        ),
        grid_spec=pltpu.PrefetchScalarGridSpec(
            num_scalar_prefetch=3,
            grid=(fine // ROWS,),
            in_specs=[
                pl.BlockSpec((ROWS, per_row, width, width), lambda g, *_: (g, 0, 0, 0)),
                whole((fine, width, width)),
                whole((half, width, lanes)),
                whole((half, width, lanes)),
            ],
            out_specs=(whole((chips, share, lanes)), whole((chips, share, lanes))),
            scratch_shapes=[
                pltpu.VMEM((3 * fine, width, lanes), BF16),
                pltpu.VMEM((n_tiles * width, lanes), F32),
            ],
        ),
        name="galerkin",
    )(core, cols, tiles, a_blocks[0], own, before, after)

    other = lax.ppermute(send, "sub", swap)
    merged = (keep + other.astype(F32)).astype(BF16)
    got = lax.all_to_all(merged, "sub", 0, 0, axis_index_groups=columns, tiled=True)
    block = pl.pallas_call(
        finish,
        out_shape=jax.ShapeDtypeStruct((chips, share, lanes), BF16),
        scratch_shapes=[pltpu.VMEM((share, lanes), F32)],
        compiler_params=pltpu.CompilerParams(vmem_limit_bytes=8 << 20),
        name="finish",
    )(got)
    mine = lax.all_to_all(block, "sub", 0, 0, axis_index_groups=columns, tiled=True)
    theirs = lax.ppermute(mine, "sub", swap)
    anywhere = pl.BlockSpec(memory_space=pl.ANY)
    out = pl.pallas_call(
        spread,
        out_shape=jax.ShapeDtypeStruct((width * width, n_tiles), BF16),
        in_specs=[anywhere, anywhere],
        out_specs=anywhere,
        scratch_shapes=[
            pltpu.VMEM((chips, share, lanes), BF16),
            pltpu.VMEM((chips, share, lanes), BF16),
            pltpu.VMEM((width * width, n_tiles), BF16),
            pltpu.SemaphoreType.DMA((2, chips)),
            pltpu.SemaphoreType.DMA((chips,)),
        ],
        compiler_params=pltpu.CompilerParams(vmem_limit_bytes=12 << 20),
        name="spread",
    )(mine, theirs)
    return out.reshape(width, width, n_tiles).transpose(2, 0, 1)[None]


def solution(mesh):
    placed = (
        P("dom", "sub", None, None, None),
        P("dom", "sub", None, None),
        P("dom", "sub", None),
        P("dom", "sub", None),
    )
    n_tiles = 12 * mesh.shape["sub"]
    return jax.shard_map(
        functools.partial(body, n_tiles),
        mesh=mesh,
        in_specs=placed,
        out_specs=P("dom", None, None, None),
        check_vma=False,
    )
```

```python
import functools

import jax
import jax.numpy as jnp
from jax import lax
from jax.experimental import pallas as pl
from jax.experimental.pallas import tpu as pltpu
from jax.sharding import PartitionSpec as P

F32, BF16 = jnp.float32, jnp.bfloat16
ROWS = 8
SPAN = 8
GROUP = 2
GRANT = 8


def twice(x):
    return jnp.concatenate([x, x], axis=-1)


def project(p_ref, a_ref, pa_ref, near_ref, acc_ref):
    fine, width = p_ref.shape[0], p_ref.shape[1]
    steps, clear = fine // ROWS, acc_ref.shape[0] // fine

    def step(g, _):
        for r in range(ROWS):
            i = g * ROWS + r
            left = p_ref[i].T
            for k in range(a_ref.shape[1]):
                pa_ref[i, k] = jnp.dot(left, a_ref[i, k], preferred_element_type=F32).astype(BF16)
            near_ref[fine + i] = twice(p_ref[i])
            at = pl.ds(pl.multiple_of(i * clear, width), clear)
            acc_ref[at, :] = jnp.zeros((clear, 2 * width), F32)
        return 0

    lax.fori_loop(0, steps, step, 0)


def galerkin(cols, tiles, pa, before_ref, after_ref, near_in, acc_in, keep_ref, send_ref, near, acc):
    fine, per_row, width = pa.shape[0], pa.shape[1], pa.shape[2]
    half, n_tiles = fine // 2, acc.shape[0] // width

    def fill(r, _):
        for start, ref in ((0, before_ref), (2 * fine, after_ref)):
            both = ref[r]
            near[start + r] = twice(both[:, :width])
            near[start + half + r] = twice(both[:, width:])
        return 0

    lax.fori_loop(0, half, fill, 0, unroll=4)

    def add(i, group, terms):
        ids = [tiles[k, i] for k in group]
        at = [pl.ds(pl.multiple_of(t * width, width), width) for t in ids]
        found, sums = [acc[rows, :] for rows in at], []
        for n, term in enumerate(terms):
            base = found[n]
            for m in range(n):
                base = jnp.where(ids[m] == ids[n], sums[m], base)
            sums.append(base + term)
        for rows, value in zip(at, sums):
            acc[rows, :] = value

    def step(g, _):
        for r in range(SPAN):
            i = g * SPAN + r
            terms = [
                jnp.dot(pa[i, k], near[cols[k, i]], preferred_element_type=F32) for k in range(per_row)
            ]
            for k in range(0, per_row, GROUP):
                add(i, range(k, k + GROUP), terms[k : k + GROUP])
        return 0

    lax.fori_loop(0, fine // SPAN, step, 0)

    first_core = lax.broadcasted_iota(jnp.int32, (8, 2 * width), 0) * 0 + lax.axis_index("sub") % 2 == 0
    left_half = lax.broadcasted_iota(jnp.int32, (8, 2 * width), 1) < width
    upper = lax.broadcasted_iota(jnp.int32, (8, 2 * width), 0) < 4
    groups, quads = keep_ref.shape[0], n_tiles // 4

    def pack(u, _):
        for y in range(groups):
            rows = []
            for w in range(2):

                def tile(q):
                    start = (2 * u + w + q * quads) * width + 8 * y
                    return acc[pl.ds(pl.multiple_of(start, 8), 8), :]

                even = jnp.where(left_half, tile(0), tile(2))
                odd = jnp.where(left_half, tile(1), tile(3))
                top = jnp.where(upper, even, pltpu.roll(odd, 4, 0))
                bottom = jnp.where(upper, pltpu.roll(even, 4, 0), odd)
                rows.append((jnp.where(first_core, top, bottom), jnp.where(first_core, bottom, top)))
            at = pl.ds(pl.multiple_of(16 * u, 16), 16)
            keep_ref[y, at, :] = jnp.concatenate([rows[0][0], rows[1][0]], axis=0)
            send_ref[y, at, :] = jnp.concatenate([rows[0][1], rows[1][1]], axis=0).astype(BF16)
        return 0

    lax.fori_loop(0, quads // 2, pack, 0, unroll=2)


def finish(got_ref, out_ref, total):
    peers, packed, lanes = got_ref.shape
    half, quads = lanes // 2, packed // 8
    n_tiles = 4 * quads
    sums = got_ref[0].astype(F32)
    for y in range(1, peers):
        sums = sums + got_ref[y].astype(F32)
    total[...] = sums
    slab = []
    for r in range(4):
        rows = [total[pl.ds(4 * s + r, quads, stride=8), :] for s in range(2)]
        turned = jnp.concatenate(rows, axis=0).T
        slab.append(jnp.concatenate([turned[:half], turned[half:]], axis=1))
    slab = jnp.concatenate(slab, axis=0)
    rest = jnp.concatenate([slab[:lanes, lanes:], slab[lanes:, lanes:]], axis=1)
    block = jnp.concatenate([slab[:, :lanes], rest], axis=0).astype(BF16)
    for y in range(peers):
        out_ref[y] = block


def spread(mine, other, out_hbm, out, sems):
    core = lax.axis_index("sub") % 2
    chips, packed, lanes = mine.shape
    slab, half = out.shape[0] // (2 * chips), lanes // 2

    def put(y):
        rows = pl.ds(2 * slab * y, 2 * slab)
        return pltpu.make_async_copy(out.at[rows], out_hbm.at[rows], sems.at[y])

    for y in range(chips):
        for ref, at in ((mine, core), (other, 1 - core)):
            start = pl.multiple_of((2 * y + at) * slab, slab)
            out[pl.ds(start, slab), 0:lanes] = ref[y, 0:slab, :]
            rest = ref[y, slab:packed, :]
            out[pl.ds(start, lanes), lanes : lanes + half] = rest[:, :half]
            out[pl.ds(start + lanes, lanes), lanes : lanes + half] = rest[:, half:]
        put(y).start()
    for y in range(chips):
        put(y).wait()


def body(n_tiles, a_blocks, p_blocks, a_cols, tile_of_item):
    fine, per_row, width = a_blocks.shape[1], a_blocks.shape[2], a_blocks.shape[3]
    subs, doms = lax.axis_size("sub"), lax.axis_size("dom")
    chips = subs // 2
    lanes = 2 * width
    half = fine // 2
    own = p_blocks[0]
    cols, tiles = a_cols[0].T, tile_of_item[0].T

    up = [(d, d + 1) for d in range(doms - 1)]
    down = [(d + 1, d) for d in range(doms - 1)]
    swap = [(s, s ^ 1) for s in range(subs)]
    columns = [[2 * y + c for y in range(chips)] for c in range(2)]

    packed = jnp.concatenate([own[:half], own[half:]], axis=-1)
    before = lax.ppermute(packed, "dom", up)
    after = lax.ppermute(packed, "dom", down)

    smem = pl.BlockSpec(memory_space=pltpu.SMEM)
    vmem = pl.BlockSpec(memory_space=pltpu.VMEM)
    anywhere = pl.BlockSpec(memory_space=pl.ANY)
    blocks = jax.ShapeDtypeStruct((fine, per_row, width, width), BF16)
    near = jax.ShapeDtypeStruct((3 * fine, width, lanes), BF16)
    sums = jax.ShapeDtypeStruct((n_tiles * width, lanes), F32)
    projected, own_near, clear = pl.pallas_call(
        project,
        out_shape=(blocks, near, sums),
        in_specs=[vmem, vmem],
        out_specs=(vmem, vmem, vmem),
        compiler_params=pltpu.CompilerParams(vmem_limit_bytes=GRANT << 20),
        cost_estimate=pl.CostEstimate(
            flops=fine * per_row * 2 * lanes**3, bytes_accessed=4 * a_blocks.size, transcendentals=0
        ),
        name="project",
    )(own, a_blocks[0])

    share = width // subs // 2 * n_tiles
    keep, send, _, _ = pl.pallas_call(
        galerkin,
        out_shape=(
            jax.ShapeDtypeStruct((chips, share, lanes), F32),
            jax.ShapeDtypeStruct((chips, share, lanes), BF16),
            near,
            sums,
        ),
        in_specs=[smem, smem, vmem, vmem, vmem, vmem, vmem],
        out_specs=(vmem, vmem, vmem, vmem),
        input_output_aliases={5: 2, 6: 3},
        compiler_params=pltpu.CompilerParams(vmem_limit_bytes=GRANT << 20),
        name="galerkin",
    )(cols, tiles, projected, before, after, own_near, clear)

    other = lax.ppermute(send, "sub", swap)
    merged = (keep + other.astype(F32)).astype(BF16)
    got = lax.all_to_all(merged, "sub", 0, 0, axis_index_groups=columns, tiled=True)
    block = pl.pallas_call(
        finish,
        out_shape=jax.ShapeDtypeStruct((chips, share, lanes), BF16),
        scratch_shapes=[pltpu.VMEM((share, lanes), F32)],
        compiler_params=pltpu.CompilerParams(vmem_limit_bytes=8 << 20),
        name="finish",
    )(got)
    mine = lax.all_to_all(block, "sub", 0, 0, axis_index_groups=columns, tiled=True)
    theirs = lax.ppermute(mine, "sub", swap)
    out = pl.pallas_call(
        spread,
        out_shape=jax.ShapeDtypeStruct((width * width, n_tiles), BF16),
        in_specs=[vmem, vmem],
        out_specs=anywhere,
        scratch_shapes=[pltpu.VMEM((width * width, n_tiles), BF16), pltpu.SemaphoreType.DMA((chips,))],
        compiler_params=pltpu.CompilerParams(vmem_limit_bytes=8 << 20),
        name="spread",
    )(mine, theirs)
    return out.reshape(width, width, n_tiles).transpose(2, 0, 1)[None]


def solution(mesh):
    placed = (
        P("dom", "sub", None, None, None),
        P("dom", "sub", None, None),
        P("dom", "sub", None),
        P("dom", "sub", None),
    )
    n_tiles = 12 * mesh.shape["sub"]
    return jax.shard_map(
        functools.partial(body, n_tiles),
        mesh=mesh,
        in_specs=placed,
        out_specs=P("dom", None, None, None),
        check_vma=False,
    )
```

```python
import functools

import jax
import jax.numpy as jnp
from jax import lax
from jax.experimental import pallas as pl
from jax.experimental.pallas import tpu as pltpu
from jax.sharding import PartitionSpec as P

F32, BF16 = jnp.float32, jnp.bfloat16
ROWS = 8
SPAN = 8
GROUP = 2
GRANT = 8


def twice(x):
    return jnp.concatenate([x, x], axis=-1)


def project(p_ref, a_ref, pa_ref, near_ref, acc_ref):
    fine, width = p_ref.shape[0], p_ref.shape[1]
    steps, clear = fine // ROWS, acc_ref.shape[0] // fine

    def step(g, _):
        for r in range(ROWS):
            i = g * ROWS + r
            left = p_ref[i].T
            for k in range(a_ref.shape[1]):
                pa_ref[i, k] = jnp.dot(left, a_ref[i, k], preferred_element_type=F32).astype(BF16)
            near_ref[fine + i] = twice(p_ref[i])
            at = pl.ds(pl.multiple_of(i * clear, width), clear)
            acc_ref[at, :] = jnp.zeros((clear, 2 * width), F32)
        return 0

    lax.fori_loop(0, steps, step, 0)


def galerkin(cols, tiles, pa, pair_ref, cross_ref, near_in, acc_in, keep_ref, send_ref, near, acc):
    fine, per_row, width = pa.shape[0], pa.shape[1], pa.shape[2]
    half, n_tiles = fine // 2, acc.shape[0] // width

    after = 2 * fine * (lax.axis_index("dom") % 2)

    def fill(r, _):
        for start, ref in ((2 * fine - after, pair_ref), (after, cross_ref)):
            both = ref[r]
            near[start + r] = twice(both[:, :width])
            near[start + half + r] = twice(both[:, width:])
        return 0

    lax.fori_loop(0, half, fill, 0, unroll=4)

    def add(i, group, terms):
        ids = [tiles[k, i] for k in group]
        at = [pl.ds(pl.multiple_of(t * width, width), width) for t in ids]
        found, sums = [acc[rows, :] for rows in at], []
        for n, term in enumerate(terms):
            base = found[n]
            for m in range(n):
                base = jnp.where(ids[m] == ids[n], sums[m], base)
            sums.append(base + term)
        for rows, value in zip(at, sums):
            acc[rows, :] = value

    def step(g, _):
        for r in range(SPAN):
            i = g * SPAN + r
            terms = [
                jnp.dot(pa[i, k], near[cols[k, i]], preferred_element_type=F32) for k in range(per_row)
            ]
            for k in range(0, per_row, GROUP):
                add(i, range(k, k + GROUP), terms[k : k + GROUP])
        return 0

    lax.fori_loop(0, fine // SPAN, step, 0)

    first_core = lax.broadcasted_iota(jnp.int32, (8, 2 * width), 0) * 0 + lax.axis_index("sub") % 2 == 0
    left_half = lax.broadcasted_iota(jnp.int32, (8, 2 * width), 1) < width
    upper = lax.broadcasted_iota(jnp.int32, (8, 2 * width), 0) < 4
    groups, quads = keep_ref.shape[0], n_tiles // 4

    def pack(u, _):
        for y in range(groups):
            rows = []
            for w in range(2):

                def tile(q):
                    start = (2 * u + w + q * quads) * width + 8 * y
                    return acc[pl.ds(pl.multiple_of(start, 8), 8), :]

                even = jnp.where(left_half, tile(0), tile(2))
                odd = jnp.where(left_half, tile(1), tile(3))
                top = jnp.where(upper, even, pltpu.roll(odd, 4, 0))
                bottom = jnp.where(upper, pltpu.roll(even, 4, 0), odd)
                rows.append((jnp.where(first_core, top, bottom), jnp.where(first_core, bottom, top)))
            at = pl.ds(pl.multiple_of(16 * u, 16), 16)
            keep_ref[y, at, :] = jnp.concatenate([rows[0][0], rows[1][0]], axis=0)
            send_ref[y, at, :] = jnp.concatenate([rows[0][1], rows[1][1]], axis=0).astype(BF16)
        return 0

    lax.fori_loop(0, quads // 2, pack, 0, unroll=2)


def finish(got_ref, out_ref, total):
    peers, packed, lanes = got_ref.shape
    half, quads = lanes // 2, packed // 8
    n_tiles = 4 * quads
    sums = got_ref[0].astype(F32)
    for y in range(1, peers):
        sums = sums + got_ref[y].astype(F32)
    total[...] = sums
    slab = []
    for r in range(4):
        rows = [total[pl.ds(4 * s + r, quads, stride=8), :] for s in range(2)]
        turned = jnp.concatenate(rows, axis=0).T
        slab.append(jnp.concatenate([turned[:half], turned[half:]], axis=1))
    slab = jnp.concatenate(slab, axis=0)
    rest = jnp.concatenate([slab[:lanes, lanes:], slab[lanes:, lanes:]], axis=1)
    block = jnp.concatenate([slab[:, :lanes], rest], axis=0).astype(BF16)
    for y in range(peers):
        out_ref[y] = block


def spread(mine, other, out_hbm, out, sems):
    core = lax.axis_index("sub") % 2
    chips, packed, lanes = mine.shape
    slab, half = out.shape[0] // (2 * chips), lanes // 2

    def put(y):
        rows = pl.ds(2 * slab * y, 2 * slab)
        return pltpu.make_async_copy(out.at[rows], out_hbm.at[rows], sems.at[y])

    for y in range(chips):
        for ref, at in ((mine, core), (other, 1 - core)):
            start = pl.multiple_of((2 * y + at) * slab, slab)
            out[pl.ds(start, slab), 0:lanes] = ref[y, 0:slab, :]
            rest = ref[y, slab:packed, :]
            out[pl.ds(start, lanes), lanes : lanes + half] = rest[:, :half]
            out[pl.ds(start + lanes, lanes), lanes : lanes + half] = rest[:, half:]
        put(y).start()
    for y in range(chips):
        put(y).wait()


def body(n_tiles, a_blocks, p_blocks, a_cols, tile_of_item):
    fine, per_row, width = a_blocks.shape[1], a_blocks.shape[2], a_blocks.shape[3]
    subs, doms = lax.axis_size("sub"), lax.axis_size("dom")
    chips = subs // 2
    lanes = 2 * width
    half = fine // 2
    own = p_blocks[0]
    cols, tiles = a_cols[0].T, tile_of_item[0].T

    pairs = [(d, d ^ 1) for d in range(doms)]
    crossed = [(d, d + 1 if d % 2 else d - 1) for d in range(1, doms - 1)]
    swap = [(s, s ^ 1) for s in range(subs)]
    columns = [[2 * y + c for y in range(chips)] for c in range(2)]

    packed = jnp.concatenate([own[:half], own[half:]], axis=-1)
    pair = lax.ppermute(packed, "dom", pairs)
    cross = lax.ppermute(packed, "dom", crossed)

    smem = pl.BlockSpec(memory_space=pltpu.SMEM)
    vmem = pl.BlockSpec(memory_space=pltpu.VMEM)
    anywhere = pl.BlockSpec(memory_space=pl.ANY)
    blocks = jax.ShapeDtypeStruct((fine, per_row, width, width), BF16)
    near = jax.ShapeDtypeStruct((3 * fine, width, lanes), BF16)
    sums = jax.ShapeDtypeStruct((n_tiles * width, lanes), F32)
    projected, own_near, clear = pl.pallas_call(
        project,
        out_shape=(blocks, near, sums),
        in_specs=[vmem, vmem],
        out_specs=(vmem, vmem, vmem),
        compiler_params=pltpu.CompilerParams(vmem_limit_bytes=GRANT << 20),
        cost_estimate=pl.CostEstimate(
            flops=fine * per_row * 2 * lanes**3, bytes_accessed=4 * a_blocks.size, transcendentals=0
        ),
        name="project",
    )(own, a_blocks[0])

    share = width // subs // 2 * n_tiles
    keep, send, _, _ = pl.pallas_call(
        galerkin,
        out_shape=(
            jax.ShapeDtypeStruct((chips, share, lanes), F32),
            jax.ShapeDtypeStruct((chips, share, lanes), BF16),
            near,
            sums,
        ),
        in_specs=[smem, smem, vmem, vmem, vmem, vmem, vmem],
        out_specs=(vmem, vmem, vmem, vmem),
        input_output_aliases={5: 2, 6: 3},
        compiler_params=pltpu.CompilerParams(vmem_limit_bytes=GRANT << 20),
        name="galerkin",
    )(cols, tiles, projected, pair, cross, own_near, clear)

    other = lax.ppermute(send, "sub", swap)
    merged = (keep + other.astype(F32)).astype(BF16)
    got = lax.all_to_all(merged, "sub", 0, 0, axis_index_groups=columns, tiled=True)
    block = pl.pallas_call(
        finish,
        out_shape=jax.ShapeDtypeStruct((chips, share, lanes), BF16),
        scratch_shapes=[pltpu.VMEM((share, lanes), F32)],
        compiler_params=pltpu.CompilerParams(vmem_limit_bytes=8 << 20),
        name="finish",
    )(got)
    mine = lax.all_to_all(block, "sub", 0, 0, axis_index_groups=columns, tiled=True)
    theirs = lax.ppermute(mine, "sub", swap)
    out = pl.pallas_call(
        spread,
        out_shape=jax.ShapeDtypeStruct((width * width, n_tiles), BF16),
        in_specs=[vmem, vmem],
        out_specs=anywhere,
        scratch_shapes=[pltpu.VMEM((width * width, n_tiles), BF16), pltpu.SemaphoreType.DMA((chips,))],
        compiler_params=pltpu.CompilerParams(vmem_limit_bytes=8 << 20),
        name="spread",
    )(mine, theirs)
    return out.reshape(width, width, n_tiles).transpose(2, 0, 1)[None]


def solution(mesh):
    placed = (
        P("dom", "sub", None, None, None),
        P("dom", "sub", None, None),
        P("dom", "sub", None),
        P("dom", "sub", None),
    )
    n_tiles = 12 * mesh.shape["sub"]
    return jax.shard_map(
        functools.partial(body, n_tiles),
        mesh=mesh,
        in_specs=placed,
        out_specs=P("dom", None, None, None),
        check_vma=False,
    )
```

```python
import functools

import jax
import jax.numpy as jnp
from jax import lax
from jax.experimental import pallas as pl
from jax.experimental.pallas import tpu as pltpu
from jax.sharding import PartitionSpec as P


F32, BF16 = jnp.float32, jnp.bfloat16
ROWS = 8
SPAN = 8
GROUP = 2
DEPTH = 8
GRANT = 8


def twice(x):
    return jnp.concatenate([x, x], axis=-1)


def project(p_ref, a_ref, pa_ref, near_ref, acc_ref):
    fine, width = p_ref.shape[0], p_ref.shape[1]
    steps, clear = fine // ROWS, acc_ref.shape[0] // fine

    def step(g, _):
        for r in range(ROWS):
            i = g * ROWS + r
            left = p_ref[i].T
            for k in range(a_ref.shape[1]):
                pa_ref[i, k] = jnp.dot(left, a_ref[i, k], preferred_element_type=F32).astype(BF16)
            near_ref[fine + i] = twice(p_ref[i])
            at = pl.ds(pl.multiple_of(i * clear, width), clear)
            acc_ref[at, :] = jnp.zeros((clear, 2 * width), F32)
        return 0

    lax.fori_loop(0, steps, step, 0)


def galerkin(cols, tiles, pa, early_ref, cross_ref, late_ref, near_in, acc_in, keep_ref, send_ref, near, acc):
    fine, per_row, width = pa.shape[0], pa.shape[1], pa.shape[2]
    half, n_tiles = fine // 2, acc.shape[0] // width

    after = 2 * fine * (lax.axis_index("dom") % 2)

    def fill(r, _):
        pair = early_ref[r] + late_ref[r]
        for start, both in ((2 * fine - after, pair), (after, cross_ref[r])):
            near[start + r] = twice(both[:, :width])
            near[start + half + r] = twice(both[:, width:])
        return 0

    lax.fori_loop(0, half, fill, 0, unroll=4)

    def add(i, group, terms):
        ids = [tiles[k, i] for k in group]
        at = [pl.ds(pl.multiple_of(t * width, width), width) for t in ids]
        found, sums = [acc[rows, :] for rows in at], []
        for n, term in enumerate(terms):
            base = found[n]
            for m in range(n):
                base = jnp.where(ids[m] == ids[n], sums[m], base)
            sums.append(base + term)
        for rows, value in zip(at, sums):
            acc[rows, :] = value

    def step(g, _):
        for r in range(SPAN):
            i = g * SPAN + r
            terms = [
                jnp.dot(pa[i, k], near[cols[k, i]], preferred_element_type=F32) for k in range(per_row)
            ]
            for k in range(0, per_row, GROUP):
                add(i, range(k, k + GROUP), terms[k : k + GROUP])
        return 0

    lax.fori_loop(0, fine // SPAN, step, 0)

    first_core = lax.broadcasted_iota(jnp.int32, (8, 2 * width), 0) * 0 + lax.axis_index("sub") % 2 == 0
    left_half = lax.broadcasted_iota(jnp.int32, (8, 2 * width), 1) < width
    upper = lax.broadcasted_iota(jnp.int32, (8, 2 * width), 0) < 4
    groups, quads = keep_ref.shape[0], n_tiles // 4

    def pack(u, _):
        for y in range(groups):
            rows = []
            for w in range(2):

                def tile(q):
                    start = (2 * u + w + q * quads) * width + 8 * y
                    return acc[pl.ds(pl.multiple_of(start, 8), 8), :]

                even = jnp.where(left_half, tile(0), tile(2))
                odd = jnp.where(left_half, tile(1), tile(3))
                top = jnp.where(upper, even, pltpu.roll(odd, 4, 0))
                bottom = jnp.where(upper, pltpu.roll(even, 4, 0), odd)
                rows.append((jnp.where(first_core, top, bottom), jnp.where(first_core, bottom, top)))
            at = pl.ds(pl.multiple_of(16 * u, 16), 16)
            keep_ref[y, at, :] = jnp.concatenate([rows[0][0], rows[1][0]], axis=0)
            send_ref[y, at, :] = jnp.concatenate([rows[0][1], rows[1][1]], axis=0).astype(BF16)
        return 0

    lax.fori_loop(0, quads // 2, pack, 0, unroll=2)


def finish(got_ref, out_ref, total):
    peers, packed, lanes = got_ref.shape
    half, quads = lanes // 2, packed // 8
    sums = got_ref[0].astype(F32)
    for y in range(1, peers):
        sums = sums + got_ref[y].astype(F32)
    total[...] = sums
    slab = []
    for r in range(4):
        rows = [total[pl.ds(4 * s + r, quads, stride=8), :] for s in range(2)]
        turned = jnp.concatenate(rows, axis=0).T
        slab.append(jnp.concatenate([turned[:half], turned[half:]], axis=1))
    slab = jnp.concatenate(slab, axis=0)
    rest = jnp.concatenate([slab[:lanes, lanes:], slab[lanes:, lanes:]], axis=1)
    block = jnp.concatenate([slab[:, :lanes], rest], axis=0).astype(BF16)
    for y in range(peers):
        out_ref[y] = block


def spread(mine, other, out_hbm, out, sems):
    core = lax.axis_index("sub") % 2
    chips, packed, lanes = mine.shape
    slab, half = out.shape[0] // (2 * chips), lanes // 2

    def put(y):
        rows = pl.ds(2 * slab * y, 2 * slab)
        return pltpu.make_async_copy(out.at[rows], out_hbm.at[rows], sems.at[y])

    for y in range(chips):
        for ref, at in ((mine, core), (other, 1 - core)):
            start = pl.multiple_of((2 * y + at) * slab, slab)
            out[pl.ds(start, slab), 0:lanes] = ref[y, 0:slab, :]
            rest = ref[y, slab:packed, :]
            out[pl.ds(start, lanes), lanes : lanes + half] = rest[:, :half]
            out[pl.ds(start + lanes, lanes), lanes : lanes + half] = rest[:, half:]
        put(y).start()
    for y in range(chips):
        put(y).wait()


def body(n_tiles, a_blocks, p_blocks, a_cols, tile_of_item):
    fine, per_row, width = a_blocks.shape[1], a_blocks.shape[2], a_blocks.shape[3]
    subs, doms = lax.axis_size("sub"), lax.axis_size("dom")
    chips = subs // 2
    lanes = 2 * width
    half = fine // 2
    own = p_blocks[0]
    cols, tiles = a_cols[0].T, tile_of_item[0].T

    early = [(d, d ^ 1) for d in range(doms) if d % DEPTH < 2]
    crossed = [(d, d + 1 if d % 2 else d - 1) for d in range(1, doms - 1)]
    late = [(d, d ^ 1) for d in range(doms) if d % DEPTH >= 2]
    swap = [(s, s ^ 1) for s in range(subs)]
    columns = [[2 * y + c for y in range(chips)] for c in range(2)]

    packed = jnp.concatenate([own[:half], own[half:]], axis=-1)
    early = lax.ppermute(packed, "dom", early)
    cross = lax.ppermute(packed, "dom", crossed)
    late = lax.ppermute(packed, "dom", late)

    smem = pl.BlockSpec(memory_space=pltpu.SMEM)
    vmem = pl.BlockSpec(memory_space=pltpu.VMEM)
    anywhere = pl.BlockSpec(memory_space=pl.ANY)
    blocks = jax.ShapeDtypeStruct((fine, per_row, width, width), BF16)
    near = jax.ShapeDtypeStruct((3 * fine, width, lanes), BF16)
    sums = jax.ShapeDtypeStruct((n_tiles * width, lanes), F32)
    projected, own_near, clear = pl.pallas_call(
        project,
        out_shape=(blocks, near, sums),
        in_specs=[vmem, vmem],
        out_specs=(vmem, vmem, vmem),
        compiler_params=pltpu.CompilerParams(vmem_limit_bytes=GRANT << 20),
        cost_estimate=pl.CostEstimate(
            flops=fine * per_row * 2 * lanes**3, bytes_accessed=4 * a_blocks.size, transcendentals=0
        ),
        name="project",
    )(own, a_blocks[0])

    share = width // subs // 2 * n_tiles
    keep, send, _, _ = pl.pallas_call(
        galerkin,
        out_shape=(
            jax.ShapeDtypeStruct((chips, share, lanes), F32),
            jax.ShapeDtypeStruct((chips, share, lanes), BF16),
            near,
            sums,
        ),
        in_specs=[smem, smem] + [vmem] * 6,
        out_specs=(vmem, vmem, vmem, vmem),
        input_output_aliases={6: 2, 7: 3},
        compiler_params=pltpu.CompilerParams(vmem_limit_bytes=GRANT << 20),
        name="galerkin",
    )(cols, tiles, projected, early, cross, late, own_near, clear)

    other = lax.ppermute(send, "sub", swap)
    merged = (keep + other.astype(F32)).astype(BF16)
    got = lax.all_to_all(merged, "sub", 0, 0, axis_index_groups=columns, tiled=True)
    block = pl.pallas_call(
        finish,
        out_shape=jax.ShapeDtypeStruct((chips, share, lanes), BF16),
        scratch_shapes=[pltpu.VMEM((share, lanes), F32)],
        compiler_params=pltpu.CompilerParams(vmem_limit_bytes=8 << 20),
        name="finish",
    )(got)
    mine = lax.all_to_all(block, "sub", 0, 0, axis_index_groups=columns, tiled=True)
    theirs = lax.ppermute(mine, "sub", swap)
    out = pl.pallas_call(
        spread,
        out_shape=jax.ShapeDtypeStruct((width * width, n_tiles), BF16),
        in_specs=[vmem, vmem],
        out_specs=anywhere,
        scratch_shapes=[pltpu.VMEM((width * width, n_tiles), BF16), pltpu.SemaphoreType.DMA((chips,))],
        compiler_params=pltpu.CompilerParams(vmem_limit_bytes=8 << 20),
        name="spread",
    )(mine, theirs)
    return out.reshape(width, width, n_tiles).transpose(2, 0, 1)[None]


def solution(mesh):
    placed = (
        P("dom", "sub", None, None, None),
        P("dom", "sub", None, None),
        P("dom", "sub", None),
        P("dom", "sub", None),
    )
    n_tiles = 12 * mesh.shape["sub"]
    return jax.shard_map(
        functools.partial(body, n_tiles),
        mesh=mesh,
        in_specs=placed,
        out_specs=P("dom", None, None, None),
        check_vma=False,
    )
```

```python
import functools

import jax
import jax.numpy as jnp
from jax import lax
from jax.experimental import pallas as pl
from jax.experimental.pallas import tpu as pltpu
from jax.sharding import PartitionSpec as P


F32, BF16 = jnp.float32, jnp.bfloat16
ROWS = 8
SPAN = 8
GROUP = 2
DEPTH = 8
GRANT = 8


def twice(x):
    return jnp.concatenate([x, x], axis=-1)


def project(p_ref, a_ref, pa_ref, near_ref, acc_ref):
    fine, width = p_ref.shape[0], p_ref.shape[1]
    steps, clear = fine // ROWS, acc_ref.shape[0] // fine

    def step(g, _):
        for r in range(ROWS):
            i = g * ROWS + r
            left = p_ref[i].T
            for k in range(a_ref.shape[1]):
                pa_ref[i, k] = jnp.dot(left, a_ref[i, k], preferred_element_type=F32).astype(BF16)
            near_ref[fine + i] = twice(p_ref[i])
            at = pl.ds(pl.multiple_of(i * clear, width), clear)
            acc_ref[at, :] = jnp.zeros((clear, 2 * width), F32)
        return 0

    lax.fori_loop(0, steps, step, 0)


def galerkin(cols, tiles, pa, early_ref, cross_ref, late_ref, near_in, acc_in, keep_ref, send_ref, near, acc):
    fine, per_row, width = pa.shape[0], pa.shape[1], pa.shape[2]
    half, n_tiles = fine // 2, acc.shape[0] // width

    after = 2 * fine * (lax.axis_index("dom") % 2)

    def fill(r, _):
        pair = early_ref[r] + late_ref[r]
        for start, both in ((2 * fine - after, pair), (after, cross_ref[r])):
            near[start + r] = twice(both[:, :width])
            near[start + half + r] = twice(both[:, width:])
        return 0

    lax.fori_loop(0, half, fill, 0, unroll=4)

    def add(i, group, terms):
        ids = [tiles[k, i] for k in group]
        at = [pl.ds(pl.multiple_of(t * width, width), width) for t in ids]
        found, sums = [acc[rows, :] for rows in at], []
        for n, term in enumerate(terms):
            base = found[n]
            for m in range(n):
                base = jnp.where(ids[m] == ids[n], sums[m], base)
            sums.append(base + term)
        for rows, value in zip(at, sums):
            acc[rows, :] = value

    def step(g, _):
        for r in range(SPAN):
            i = g * SPAN + r
            terms = [
                jnp.dot(pa[i, k], near[cols[k, i]], preferred_element_type=F32) for k in range(per_row)
            ]
            for k in range(0, per_row, GROUP):
                add(i, range(k, k + GROUP), terms[k : k + GROUP])
        return 0

    lax.fori_loop(0, fine // SPAN, step, 0)

    first_core = lax.broadcasted_iota(jnp.int32, (8, 2 * width), 0) * 0 + lax.axis_index("sub") % 2 == 0
    left_half = lax.broadcasted_iota(jnp.int32, (8, 2 * width), 1) < width
    upper = lax.broadcasted_iota(jnp.int32, (8, 2 * width), 0) < 4
    groups, quads = keep_ref.shape[0], n_tiles // 4

    def pack(u, _):
        for y in range(groups):
            rows = []
            for w in range(2):

                def tile(q):
                    start = (2 * u + w + q * quads) * width + 8 * y
                    return acc[pl.ds(pl.multiple_of(start, 8), 8), :]

                even = jnp.where(left_half, tile(0), tile(2))
                odd = jnp.where(left_half, tile(1), tile(3))
                top = jnp.where(upper, even, pltpu.roll(odd, 4, 0))
                bottom = jnp.where(upper, pltpu.roll(even, 4, 0), odd)
                rows.append((jnp.where(first_core, top, bottom), jnp.where(first_core, bottom, top)))
            at = pl.ds(pl.multiple_of(16 * u, 16), 16)
            keep_ref[y, at, :] = jnp.concatenate([rows[0][0], rows[1][0]], axis=0)
            send_ref[y, at, :] = jnp.concatenate([rows[0][1], rows[1][1]], axis=0).astype(BF16)
        return 0

    lax.fori_loop(0, quads // 2, pack, 0, unroll=2)


def finish(got_ref, out_ref, total):
    peers, packed, lanes = got_ref.shape
    half, quads = lanes // 2, packed // 8
    sums = got_ref[0].astype(F32)
    for y in range(1, peers):
        sums = sums + got_ref[y].astype(F32)
    total[...] = sums
    slab = []
    for r in range(4):
        rows = [total[pl.ds(4 * s + r, quads, stride=8), :] for s in range(2)]
        turned = jnp.concatenate(rows, axis=0).T
        slab.append(jnp.concatenate([turned[:half], turned[half:]], axis=1))
    slab = jnp.concatenate(slab, axis=0)
    rest = jnp.concatenate([slab[:lanes, lanes:], slab[lanes:, lanes:]], axis=1)
    block = jnp.concatenate([slab[:, :lanes], rest], axis=0).astype(BF16)
    for y in range(peers):
        out_ref[y] = block


def spread(first, second, mine, other, out_hbm, out, sems):
    core = lax.min(first[0], second[0])
    chips, packed, lanes = mine.shape
    slab, half = out.shape[0] // (2 * chips), lanes // 2

    def put(y):
        rows = pl.ds(2 * slab * y, 2 * slab)
        return pltpu.make_async_copy(out.at[rows], out_hbm.at[rows], sems.at[y])

    for y in range(chips):
        for ref, at in ((mine, core), (other, 1 - core)):
            start = pl.multiple_of((2 * y + at) * slab, slab)
            out[pl.ds(start, slab), 0:lanes] = ref[y, 0:slab, :]
            rest = ref[y, slab:packed, :]
            out[pl.ds(start, lanes), lanes : lanes + half] = rest[:, :half]
            out[pl.ds(start + lanes, lanes), lanes : lanes + half] = rest[:, half:]
        put(y).start()
    for y in range(chips):
        put(y).wait()


def body(n_tiles, a_blocks, p_blocks, a_cols, tile_of_item):
    fine, per_row, width = a_blocks.shape[1], a_blocks.shape[2], a_blocks.shape[3]
    subs, doms = lax.axis_size("sub"), lax.axis_size("dom")
    chips = subs // 2
    lanes = 2 * width
    half = fine // 2
    own = p_blocks[0]
    cols, tiles = a_cols[0].T, tile_of_item[0].T

    early = [(d, d ^ 1) for d in range(doms) if d % DEPTH < 2]
    crossed = [(d, d + 1 if d % 2 else d - 1) for d in range(1, doms - 1)]
    late = [(d, d ^ 1) for d in range(doms) if d % DEPTH >= 2]
    swap = [(s, s ^ 1) for s in range(subs)]
    columns = [[2 * y + c for y in range(chips)] for c in range(2)]

    packed = jnp.concatenate([own[:half], own[half:]], axis=-1)
    early = lax.ppermute(packed, "dom", early)
    cross = lax.ppermute(packed, "dom", crossed)
    late = lax.ppermute(packed, "dom", late)

    smem = pl.BlockSpec(memory_space=pltpu.SMEM)
    vmem = pl.BlockSpec(memory_space=pltpu.VMEM)
    anywhere = pl.BlockSpec(memory_space=pl.ANY)
    blocks = jax.ShapeDtypeStruct((fine, per_row, width, width), BF16)
    near = jax.ShapeDtypeStruct((3 * fine, width, lanes), BF16)
    sums = jax.ShapeDtypeStruct((n_tiles * width, lanes), F32)
    projected, own_near, clear = pl.pallas_call(
        project,
        out_shape=(blocks, near, sums),
        in_specs=[vmem, vmem],
        out_specs=(vmem, vmem, vmem),
        compiler_params=pltpu.CompilerParams(vmem_limit_bytes=GRANT << 20),
        cost_estimate=pl.CostEstimate(
            flops=fine * per_row * 2 * lanes**3, bytes_accessed=4 * a_blocks.size, transcendentals=0
        ),
        name="project",
    )(own, a_blocks[0])

    share = width // subs // 2 * n_tiles
    keep, send, _, _ = pl.pallas_call(
        galerkin,
        out_shape=(
            jax.ShapeDtypeStruct((chips, share, lanes), F32),
            jax.ShapeDtypeStruct((chips, share, lanes), BF16),
            near,
            sums,
        ),
        in_specs=[smem, smem] + [vmem] * 6,
        out_specs=(vmem, vmem, vmem, vmem),
        input_output_aliases={6: 2, 7: 3},
        compiler_params=pltpu.CompilerParams(vmem_limit_bytes=GRANT << 20),
        name="galerkin",
    )(cols, tiles, projected, early, cross, late, own_near, clear)

    other = lax.ppermute(send, "sub", swap)
    merged = (keep + other.astype(F32)).astype(BF16)
    exchange = functools.partial(
        lax.all_to_all, axis_name="sub", split_axis=0, concat_axis=0, axis_index_groups=columns, tiled=True
    )
    got = exchange(merged)
    first = lax.axis_index("sub").reshape(1) % 2
    second = lax.axis_index("sub").reshape(1) & 1
    block = pl.pallas_call(
        finish,
        out_shape=jax.ShapeDtypeStruct((chips, share, lanes), BF16),
        scratch_shapes=[pltpu.VMEM((share, lanes), F32)],
        compiler_params=pltpu.CompilerParams(vmem_limit_bytes=8 << 20),
        name="finish",
    )(got)
    mine = exchange(block)
    theirs = lax.ppermute(mine, "sub", swap)
    out = pl.pallas_call(
        spread,
        out_shape=jax.ShapeDtypeStruct((width * width, n_tiles), BF16),
        in_specs=[smem, smem, vmem, vmem],
        out_specs=anywhere,
        scratch_shapes=[pltpu.VMEM((width * width, n_tiles), BF16), pltpu.SemaphoreType.DMA((chips,))],
        compiler_params=pltpu.CompilerParams(vmem_limit_bytes=8 << 20),
        name="spread",
    )(first, second, mine, theirs)
    return out.reshape(width, width, n_tiles).transpose(2, 0, 1)[None]


def solution(mesh):
    placed = (
        P("dom", "sub", None, None, None),
        P("dom", "sub", None, None),
        P("dom", "sub", None),
        P("dom", "sub", None),
    )
    n_tiles = 12 * mesh.shape["sub"]
    return jax.shard_map(
        functools.partial(body, n_tiles),
        mesh=mesh,
        in_specs=placed,
        out_specs=P("dom", None, None, None),
        check_vma=False,
    )
```
